32 devices in a mesh: row: 4 (over y, x), col: 8 (over z, core).
Axes of the slice: x: 2, y: 2, z: 4, core: 2. Of those that a mesh axis runs over, the one named last changes fastest.
Arguments:
- amplitudes: bfloat16 [4096, 16384], P('col', 'row'), may hold values from -6 to 6
- integrals: bfloat16 [4096, 16384], P('row', 'col'), may hold values from -0.09375 to 0.09375
- tile_mask: int32 [64, 256], P(None, 'row'), may hold values from 0 to 1, as said below
- occ_energy: float32 [4], replicated, may hold values from -1 to -0.2
- virt_energy: float32 [4096], replicated, may hold values from 0.2 to 1.5
Outputs:
- update: bfloat16 [16384, 16384], P(('row', 'col'))
The draws below stay inside these ranges and needn't reach their ends.
Inputs may be any that keep to these rules, and one draw needn't show every extreme that they name: `tile_mask`: 0 drops a tile, 1 keeps it; the share of kept tiles differs strongly between groups of (ia) rows.
All inputs are finite; a program needn't handle non-finite values.
Results may differ from the reference program's by a relative error of at most 0.0049.
Values may be sent and summed in bfloat16 or wider, within the bound.
A program may use at most 192 MiB of HBM per device.

```python
import jax
import jax.numpy as jnp
from jax import lax

V = 4096
TILE = 64
NI = 4
KW = 4096
M = 16384
N_ROW = 4
N_COL = 8


def draw_tile_mask(key, part):
    tile_depth = KW // TILE
    tile_width = M // TILE
    groups = N_ROW
    depth_blocks = N_COL
    first_key, second_key = jax.random.split(jax.random.fold_in(key, 7))
    levels = jax.random.randint(first_key, (depth_blocks, groups), 0, 100)
    bounds = 20 + 70 * jnp.arange(groups, dtype=jnp.int32) // max(groups - 1, 1)
    active = (levels < bounds[None, :]).astype(jnp.int32)
    active = jnp.repeat(jnp.repeat(active, tile_depth // depth_blocks, axis=0), tile_width // groups, axis=1)
    tiles = (jax.random.randint(second_key, (tile_depth, tile_width), 0, 4) > 0).astype(jnp.int32)
    return active * tiles


def block_scale(rng, shape, cuts, least, top_value):
    loudness = 1.0
    for dim, parts in cuts:
        steps = jax.random.uniform(jax.random.fold_in(jax.random.fold_in(rng, 6), dim), (parts,), jnp.float32, least / len(cuts), top_value / len(cuts))
        loudness = loudness * jnp.repeat(jnp.exp(steps), shape[dim] // parts).reshape((-1,) + (1,) * (len(shape) - 1 - dim))
    return loudness


def noise(rng, extent, spread, most, pieces=(), kind=jnp.bfloat16):
    level = block_scale(rng, extent, pieces, -0.22, 0.18) if pieces else 1.0
    values = jax.random.normal(rng, extent, jnp.float32) * spread * level
    return jnp.minimum(jnp.maximum(values, -most), most).astype(kind)


def setup_inputs(seed: int = 0) -> dict:
    key_list = jax.random.split(jax.random.key(seed), 6)
    return {
        "amplitudes": noise(key_list[0], (KW, M), 1.0, 6.0, ((0, 8), (1, 4))),
        "integrals": noise(key_list[1], (KW, M), KW ** -0.5, 0.09375, ((0, 4), (1, 8))),
        "tile_mask": draw_tile_mask(jax.random.fold_in(key_list[5], 71), 0),
        "occ_energy": jnp.clip(jax.random.uniform(key_list[3], (NI,), jnp.float32, -1.0, -0.2), -1.0, -0.2),
        "virt_energy": jnp.clip(jax.random.uniform(key_list[4], (V,), jnp.float32, 0.2, 1.5), 0.2, 1.5),
    }


def reference(amplitudes, integrals, tile_mask, occ_energy, virt_energy):
    tile_depth, tile_width = tile_mask.shape
    keep_tiles = tile_mask.astype(jnp.bfloat16)
    masked = (amplitudes.reshape(tile_depth, TILE, tile_width, TILE) * keep_tiles[:, None, :, None]).reshape(KW, M)
    cycle_block = jnp.dot(masked.T, integrals, preferred_element_type=jnp.float32).astype(jnp.bfloat16)
    pair_gap = (virt_energy[None, :] - occ_energy[:, None]).astype(jnp.float32).reshape(M)
    block_rows = min(M, 1024)

    def mirror_block(index_block):
        offset = index_block * block_rows
        row_block = lax.dynamic_slice_in_dim(cycle_block, offset, block_rows, 0).astype(jnp.float32)
        col_block = lax.dynamic_slice_in_dim(cycle_block, offset, block_rows, 1).astype(jnp.float32).T
        gap_block = lax.dynamic_slice_in_dim(pair_gap, offset, block_rows, 0)
        return ((row_block + col_block) / (gap_block[:, None] + pair_gap[None, :])).astype(jnp.bfloat16)

    result = lax.map(mirror_block, jnp.arange(M // block_rows, dtype=jnp.int32))
    return result.reshape(M, M)
```

```python
import functools

import jax
import jax.numpy as jnp
from jax import lax
from jax.experimental import pallas as pl
from jax.experimental.pallas import tpu as pltpu
from jax.sharding import PartitionSpec as P

TILE = 64
PIECES = 2
MESH = pl.DeviceIdType.MESH


def gather_kernel(
    n_row, n_col, a_ref, i_ref, a_full, a_r, i_q, i_r, i_g,
    send_sem, local_sem, sem_a, sem_g, sem_q, sem_ar, sem_ir,
):
    r = lax.axis_index("row")
    c = lax.axis_index("col")
    chips = n_col // 2
    k = c // 2
    p = c % 2
    partner = c + 1 - 2 * p
    d = a_ref.shape[0] // PIECES
    e = i_ref.shape[0] // PIECES
    j = i_ref.shape[1]
    q = a_ref.shape[1] // n_col
    side = c // chips

    barrier = pltpu.get_barrier_semaphore()

    def greet(row, col):
        pl.semaphore_signal(barrier, inc=1, device_id=(row, col), device_id_type=MESH)

    greet(r, partner)
    count = 1 + 2 * (n_row - 1)
    for m in range(1, n_row):
        greet((r + m) % n_row, c)
        greet((r + m) % n_row, partner)

    greet(r, (c + 2) % n_col)
    greet(r, (c - 2 + n_col) % n_col)
    pl.semaphore_wait(barrier, count + 2)

    pending = []
    counts = [0, 0]

    def run(cond, body):
        if cond is None:
            body()
        else:
            pl.when(cond)(body)

    def send(src, dst, recv, row, col, cond=None):
        sem = send_sem.at[counts[0]]
        counts[0] += 1
        copy = pltpu.make_async_remote_copy(
            src_ref=src, dst_ref=dst, send_sem=sem, recv_sem=recv,
            device_id=(row, col), device_id_type=MESH,
        )
        run(cond, copy.start)
        pending.append((cond, copy.wait_send))

    def local(src, dst, cond=None):
        sem = local_sem.at[counts[1]]
        counts[1] += 1
        copy = pltpu.make_async_copy(src, dst, sem)
        run(cond, copy.start)
        pending.append((cond, copy.wait))

    def arrived(ref, sem, cond=None):
        run(cond, pltpu.make_async_copy(ref, ref, sem).wait)

    def both(x, y):
        return y if x is None else (x if y is None else jnp.logical_and(x, y))

    def a_rows(block, h):
        return pl.ds(pl.multiple_of((block * PIECES + h) * d, d), d)

    def i_rows(row, h):
        return pl.ds(pl.multiple_of((row * PIECES + h) * e, e), e)

    def i_cols(parity):
        return pl.ds(pl.multiple_of(parity * j, j), j)

    own = pl.ds(pl.multiple_of(c * q, q), q)

    def a_to_rows(src, block, h, cond=None):
        rows = a_rows(block, h)
        for m in range(1, n_row):
            send(src.at[:, own], a_r.at[m - 1, rows, :], sem_ar, (r + m) % n_row, c, cond)

    def i_out(src, block, h, cond=None):
        rows = i_rows(r, h)
        elsewhere = both(cond, block != r)
        send(src, i_q.at[rows, i_cols(p)], sem_q.at[r, p, h], block, c, elsewhere)
        here = both(cond, block == r)
        local(src, i_q.at[rows, i_cols(p)], here)
        send(src, i_q.at[rows, i_cols(p)], sem_q.at[r, p, h], r, partner, here)
        holder = both(cond, side == p)
        for t in range(2):
            col = 2 * k + t
            part = src.at[:, pl.ds(pl.multiple_of((col - side * chips) * q, q), q)]
            for m in range(1, n_row):
                row = (r + m) % n_row
                slot = (row - block + n_row) % n_row
                send(part, i_r.at[slot, rows, :], sem_ir.at[r, h], row, col, holder)
            slot = (r - block + n_row) % n_row
            send(part, i_r.at[slot, rows, :], sem_ir.at[r, h], r, partner, both(holder, p != t))
            local(part, i_r.at[slot, rows, :], both(holder, p == t))

    up, down = k < chips - 1, k > 0
    for h in range(PIECES):
        a_own = a_ref.at[pl.ds(h * d, d), :]
        i_own = i_ref.at[pl.ds(h * e, e), :]
        dst_a = a_full.at[a_rows(c, h), :]
        for cond, col in ((up, c + 2), (down, c - 2)):
            send(i_own, i_g.at[k, pl.ds(h * e, e), :], sem_g.at[k, h], r, col, cond)
            send(a_own, dst_a, sem_a.at[c, h], r, col, cond)
        i_out(i_own, k, h)
        send(a_own, dst_a, sem_a.at[c, h], r, partner)
        a_to_rows(a_own, c, h)
        local(a_own, dst_a)

    def hand_q(h, cond):
        for m in range(1, n_row):
            row = (r + m) % n_row
            piece = i_q.at[i_rows(row, h), i_cols(p)]
            arrived(piece, sem_q.at[row, p, h], cond)
            send(piece, piece, sem_q.at[row, p, h], r, partner, cond)

    for s in range(1, chips):
        for h in range(PIECES):
            for sign in (-1, 1):
                far = k + sign * s
                there = far >= 0 if sign < 0 else far < chips
                onward = both(there, up if sign < 0 else down)
                g = i_g.at[jnp.clip(far, 0, chips - 1), pl.ds(h * e, e), :]
                col = c - 2 * sign
                block = 2 * far + p
                full = a_full.at[a_rows(jnp.clip(block, 0, n_col - 1), h), :]
                got_g = sem_g.at[jnp.clip(far, 0, chips - 1), h]
                got_a = sem_a.at[jnp.clip(block, 0, n_col - 1), h]
                arrived(g, got_g, there)
                send(g, g, got_g, r, col, onward)
                i_out(g, jnp.clip(far, 0, chips - 1), h, there)
                arrived(full, got_a, there)
                send(full, full, got_a, r, col, onward)
                send(full, full, got_a, r, partner, there)
                a_to_rows(full, jnp.clip(block, 0, n_col - 1), h, there)
            for sign in (-1, 1):
                far = k + sign * (s - 1)
                if s == 1 and sign > 0:
                    continue
                there = far >= 0 if sign < 0 else far < chips
                other = jnp.clip(2 * far + 1 - p, 0, n_col - 1)
                full = a_full.at[a_rows(other, h), :]
                arrived(full, sem_a.at[other, h], there)
                a_to_rows(full, other, h, there)
            hand_q(h, jnp.logical_or(r - k == s - 1, k - r == s - 1))
    for h in range(PIECES):
        for sign in (-1, 1):
            far = k + sign * (chips - 1)
            there = far >= 0 if sign < 0 else far < chips
            other = jnp.clip(2 * far + 1 - p, 0, n_col - 1)
            full = a_full.at[a_rows(other, h), :]
            arrived(full, sem_a.at[other, h], there)
            a_to_rows(full, other, h, there)
        hand_q(h, jnp.logical_or(r - k == chips - 1, k - r == chips - 1))

    for h in range(PIECES):
        for m in range(n_row):
            row = (r + m) % n_row
            arrived(i_q.at[i_rows(row, h), i_cols(1 - p)], sem_q.at[row, 1 - p, h])
            if m:
                arrived(i_r.at[:, i_rows(row, h), :], sem_ir.at[row, h])
        arrived(i_r.at[:, i_rows(r, h), :], sem_ir.at[r, h], side != p)
    arrived(a_r, sem_ar)
    for cond, wait in pending:
        run(cond, wait)


def sem_counts(n_row, n_col):
    chips = n_col // 2
    i_out = 2 + 2 * n_row
    sends = PIECES * (5 + i_out + n_row - 1)
    steps = chips - 1
    sends += PIECES * 2 * steps * (3 + i_out + n_row - 1)
    sends += PIECES * ((2 * steps - 1) * (n_row - 1) + steps * (n_row - 1))
    sends += PIECES * 3 * (n_row - 1)
    locals_ = PIECES * (4 + 2 * steps * 3)
    return sends, locals_


def gather(n_row, n_col, a, i):
    d, w = a.shape
    e, j = i.shape
    q = w // n_col
    depth = d * n_col
    chips = n_col // 2
    sends, locals_ = sem_counts(n_row, n_col)
    dma = pltpu.SemaphoreType.DMA
    hbm = pl.BlockSpec(memory_space=pl.ANY)
    shapes = [(depth, w), (n_row - 1, depth, q), (depth, w), (n_row, depth, q), (chips, e, j)]
    return pl.pallas_call(
        functools.partial(gather_kernel, n_row, n_col),
        out_shape=[jax.ShapeDtypeStruct(s, a.dtype) for s in shapes],
        in_specs=[hbm] * 2,
        out_specs=[hbm] * 5,
        scratch_shapes=[
            dma((sends,)), dma((locals_,)), dma((n_col, PIECES)), dma((chips, PIECES)),
            dma((n_row, 2, PIECES)), dma, dma((n_row, PIECES)),
        ],
        compiler_params=pltpu.CompilerParams(collective_id=0, has_side_effects=True),
    )(a, i)


def local(amplitudes, integrals, tile_mask, occ_energy, virt_energy):
    n_row = lax.axis_size("row")
    n_col = lax.axis_size("col")
    r = lax.axis_index("row")
    c = lax.axis_index("col")
    local_depth, local_width = amplitudes.shape
    tile_rows = local_depth // TILE
    tile_cols = local_width // TILE
    own_mask = lax.dynamic_slice_in_dim(tile_mask, c * tile_rows, tile_rows, 0)
    keep_tiles = own_mask.astype(jnp.bfloat16)
    masked = (
        amplitudes.reshape(tile_rows, TILE, tile_cols, TILE) * keep_tiles[:, None, :, None]
    ).reshape(local_depth, local_width)
    a_full, a_r, i_q, i_r, _ = gather(n_row, n_col, masked, integrals)
    q = local_width // n_col
    pair_gap = (virt_energy[None, :] - occ_energy[:, None]).reshape(-1)
    col_gap = lax.dynamic_slice_in_dim(pair_gap, r * local_width, local_width, 0)
    out = jnp.zeros((q, pair_gap.shape[0]), jnp.bfloat16)
    dims = (((0,), (0,)), ((), ()))
    landed = []
    for m in [*range(1, n_row), 0]:
        target = (r - m) % n_row
        left = a_r[m - 1] if m else lax.dynamic_slice_in_dim(a_full, c * q, q, 1)
        first = lax.dot_general(left, i_q, dims, preferred_element_type=jnp.float32)
        second = lax.dot_general(i_r[m], a_full, dims, preferred_element_type=jnp.float32)
        row_gap = lax.dynamic_slice_in_dim(pair_gap, target * local_width + c * q, q, 0)
        block = ((first + second) / (row_gap[:, None] + col_gap[None, :])).astype(jnp.bfloat16)
        if m:
            block = lax.ppermute(block, "row", [(s, (s - m) % n_row) for s in range(n_row)])
        landed.append((m, block))
    for m, block in landed:
        out = lax.dynamic_update_slice_in_dim(out, block, ((r + m) % n_row) * local_width, 1)
    return out


def solution(mesh):
    return jax.shard_map(
        local,
        mesh=mesh,
        in_specs=(P("col", "row"), P("row", "col"), P(None, "row"), P(), P()),
        out_specs=P(("row", "col"), None),
        check_vma=False,
    )
```

```python
import functools

import jax
import jax.numpy as jnp
from jax import lax
from jax.experimental import pallas as pl
from jax.experimental.pallas import tpu as pltpu
from jax.sharding import PartitionSpec as P

TILE = 64
PIECES = 4
PARTS = 2
MESH = pl.DeviceIdType.MESH


def xor(u, v, n):
    total, bit = 0, 1
    while bit < n:
        total = total + (((u // bit) % 2 + (v // bit) % 2) % 2) * bit
        bit *= 2
    return total


def gather_kernel(
    n_row, n_col, a_ref, i_ref, a_full, a_r, i_q, i_r, i_g,
    send_sem, local_sem, sem_a, sem_g, sem_q, sem_ar, sem_ir,
):
    r = lax.axis_index("row")
    c = lax.axis_index("col")
    chips = n_col // 2
    k = c // 2
    p = c % 2
    partner = c + 1 - 2 * p
    d = a_ref.shape[0] // PIECES
    e = i_ref.shape[0] // PIECES
    j = i_ref.shape[1]
    q = a_ref.shape[1] // n_col
    side = c // chips

    barrier = pltpu.get_barrier_semaphore()

    def greet(row, col):
        pl.semaphore_signal(barrier, inc=1, device_id=(row, col), device_id_type=MESH)

    greet(r, partner)
    count = 1 + 2 * (n_row - 1)
    for m in range(1, n_row):
        greet(xor(r, m, n_row), c)
        greet(xor(r, m, n_row), partner)

    greet(r, (c + 2) % n_col)
    greet(r, (c - 2 + n_col) % n_col)
    pl.semaphore_wait(barrier, count + 2)

    counts = [0, 0]
    state = {"wait": False, "h": 0}

    def run(cond, body):
        if cond is None:
            body()
        else:
            pl.when(cond)(body)

    def send(src, dst, recv, row, col, cond=None):
        sem = send_sem.at[counts[0], state["h"]]
        counts[0] += 1
        copy = pltpu.make_async_remote_copy(
            src_ref=src, dst_ref=dst, send_sem=sem, recv_sem=recv,
            device_id=(row, col), device_id_type=MESH,
        )
        run(cond, copy.wait_send if state["wait"] else copy.start)

    def local(src, dst, cond=None):
        sem = local_sem.at[counts[1], state["h"]]
        counts[1] += 1
        copy = pltpu.make_async_copy(src, dst, sem)
        run(cond, copy.wait if state["wait"] else copy.start)

    def arrived(ref, sem, cond=None):
        if not state["wait"]:
            run(cond, pltpu.make_async_copy(ref, ref, sem).wait)

    def both(x, y):
        return y if x is None else (x if y is None else jnp.logical_and(x, y))

    def a_rows(block, h):
        return pl.ds(pl.multiple_of((block * PIECES + h) * d, d), d)

    def i_rows(row, h):
        return pl.ds(pl.multiple_of((row * PIECES + h) * e, e), e)

    def i_cols(parity):
        return pl.ds(pl.multiple_of(parity * j, j), j)

    own = pl.ds(pl.multiple_of(c * q, q), q)

    def a_to_rows(src, block, h, cond=None):
        rows = a_rows(block, h)
        for m in range(1, n_row):
            send(src.at[:, own], a_r.at[m - 1, rows, :], sem_ar, xor(r, m, n_row), c, cond)

    def i_out(src, block, h, cond=None):
        rows = i_rows(r, h)
        elsewhere = both(cond, block != r)
        send(src, i_q.at[rows, i_cols(p)], sem_q.at[r, p, h], block, c, elsewhere)
        here = both(cond, block == r)
        local(src, i_q.at[rows, i_cols(p)], here)
        send(src, i_q.at[rows, i_cols(p)], sem_q.at[r, p, h], r, partner, here)
        holder = both(cond, side == p)
        for t in range(2):
            col = 2 * k + t
            part = src.at[:, pl.ds(pl.multiple_of((col - side * chips) * q, q), q)]
            for m in range(1, n_row):
                row = xor(r, m, n_row)
                slot = xor(row, block, n_row)
                send(part, i_r.at[slot, rows, :], sem_ir.at[r, h], row, col, holder)
            slot = xor(r, block, n_row)
            send(part, i_r.at[slot, rows, :], sem_ir.at[r, h], r, partner, both(holder, p != t))
            local(part, i_r.at[slot, rows, :], both(holder, p == t))

    up, down = k < chips - 1, k > 0

    def hand_q(h, cond):
        for m in range(1, n_row):
            row = xor(r, m, n_row)
            piece = i_q.at[i_rows(row, h), i_cols(p)]
            arrived(piece, sem_q.at[row, p, h], cond)
            send(piece, piece, sem_q.at[row, p, h], r, partner, cond)

    def hand_other(h, sign, distance):
        far = k + sign * distance
        there = far >= 0 if sign < 0 else far < chips
        other = jnp.clip(2 * far + 1 - p, 0, n_col - 1)
        full = a_full.at[a_rows(other, h), :]
        arrived(full, sem_a.at[other, h], there)
        a_to_rows(full, other, h, there)

    def first(h):
        a_own = a_ref.at[pl.ds(pl.multiple_of(h * d, d), d), :]
        i_own = i_ref.at[pl.ds(pl.multiple_of(h * e, e), e), :]
        dst_a = a_full.at[a_rows(c, h), :]
        for cond, col in ((up, c + 2), (down, c - 2)):
            send(i_own, i_g.at[k, pl.ds(pl.multiple_of(h * e, e), e), :], sem_g.at[k, h], r, col, cond)
            send(a_own, dst_a, sem_a.at[c, h], r, col, cond)
        i_out(i_own, k, h)
        send(a_own, dst_a, sem_a.at[c, h], r, partner)
        a_to_rows(a_own, c, h)
        local(a_own, dst_a)

    def step(s, h):
        for sign in (-1, 1):
            far = k + sign * s
            there = far >= 0 if sign < 0 else far < chips
            onward = both(there, up if sign < 0 else down)
            chip = jnp.clip(far, 0, chips - 1)
            g = i_g.at[chip, pl.ds(pl.multiple_of(h * e, e), e), :]
            col = c - 2 * sign
            block = jnp.clip(2 * far + p, 0, n_col - 1)
            full = a_full.at[a_rows(block, h), :]
            arrived(g, sem_g.at[chip, h], there)
            send(g, g, sem_g.at[chip, h], r, col, onward)
            i_out(g, chip, h, there)
            arrived(full, sem_a.at[block, h], there)
            send(full, full, sem_a.at[block, h], r, col, onward)
            send(full, full, sem_a.at[block, h], r, partner, there)
            a_to_rows(full, block, h, there)
        for sign in (-1, 1) if s > 1 else (-1,):
            hand_other(h, sign, s - 1)
        hand_q(h, jnp.logical_or(r - k == s - 1, k - r == s - 1))

    def last(h):
        for sign in (-1, 1):
            hand_other(h, sign, chips - 1)
        hand_q(h, jnp.logical_or(r - k == chips - 1, k - r == chips - 1))

    phases = [first, *[functools.partial(step, s) for s in range(1, chips)], last]

    def play(wait):
        counts[:] = [0, 0]
        for phase in phases:
            base = list(counts)

            @pl.loop(0, PIECES)
            def _(h, phase=phase, base=base):
                counts[:] = base
                state.update(wait=wait, h=h)
                phase(h)

    play(False)
    state.update(wait=False)

    @pl.loop(0, PIECES)
    def _(h):
        for m in range(n_row):
            row = xor(r, m, n_row)
            arrived(i_q.at[i_rows(row, h), i_cols(1 - p)], sem_q.at[row, 1 - p, h])
            if m:
                arrived(i_r.at[:, i_rows(row, h), :], sem_ir.at[row, h])
        arrived(i_r.at[:, i_rows(r, h), :], sem_ir.at[r, h], side != p)

    arrived(a_r, sem_ar)
    play(True)


def sem_counts(n_row, n_col):
    chips = n_col // 2
    i_out = 2 + 2 * n_row
    steps = chips - 1
    sends = 5 + i_out + n_row - 1 + 2 * steps * (3 + i_out + n_row - 1)
    sends += (2 * steps - 1) * (n_row - 1) + steps * (n_row - 1) + 3 * (n_row - 1)
    locals_ = 4 + 6 * steps
    return sends, locals_


def gather(n_row, n_col, a, i):
    d, w = a.shape
    e, j = i.shape
    q = w // n_col
    depth = d * n_col
    chips = n_col // 2
    sends, locals_ = sem_counts(n_row, n_col)
    dma = pltpu.SemaphoreType.DMA
    hbm = pl.BlockSpec(memory_space=pl.ANY)
    shapes = [(depth, w), (n_row - 1, depth, q), (depth, w), (n_row, depth, q), (chips, e, j)]
    return pl.pallas_call(
        functools.partial(gather_kernel, n_row, n_col),
        out_shape=[jax.ShapeDtypeStruct(s, a.dtype) for s in shapes],
        in_specs=[hbm] * 2,
        out_specs=[hbm] * 5,
        scratch_shapes=[
            dma((sends, PIECES)), dma((locals_, PIECES)), dma((n_col, PIECES)), dma((chips, PIECES)),
            dma((n_row, 2, PIECES)), dma, dma((n_row, PIECES)),
        ],
        compiler_params=pltpu.CompilerParams(collective_id=0, has_side_effects=True),
    )(a, i)


def local(amplitudes, integrals, tile_mask, occ_energy, virt_energy):
    n_row = lax.axis_size("row")
    n_col = lax.axis_size("col")
    r = lax.axis_index("row")
    c = lax.axis_index("col")
    local_depth, local_width = amplitudes.shape
    tile_rows = local_depth // TILE
    tile_cols = local_width // TILE
    own_mask = lax.dynamic_slice_in_dim(tile_mask, c * tile_rows, tile_rows, 0)
    keep_tiles = own_mask.astype(jnp.bfloat16)
    keep = jnp.broadcast_to(keep_tiles[:, :, None], (tile_rows, tile_cols, TILE)).reshape(tile_rows, 1, local_width)
    masked = (amplitudes.reshape(tile_rows, TILE, local_width) * keep).reshape(local_depth, local_width)
    a_full, a_r, i_q, i_r, _ = gather(n_row, n_col, masked, integrals)
    q = local_width // n_col
    pair_gap = (virt_energy[None, :] - occ_energy[:, None]).reshape(-1)
    col_gap = lax.dynamic_slice_in_dim(pair_gap, r * local_width, local_width, 0)
    out = jnp.zeros((q, pair_gap.shape[0]), jnp.bfloat16)
    dims = (((0,), (0,)), ((), ()))
    landed = []
    for m in [*range(n_row - 1, 0, -1), 0]:
        target = r ^ m
        left = a_r[m - 1] if m else lax.dynamic_slice_in_dim(a_full, c * q, q, 1)
        row_gap = lax.dynamic_slice_in_dim(pair_gap, target * local_width + c * q, q, 0)
        parts = PARTS if m == n_row - 1 else 1
        part = local_width // parts
        for h in range(parts):
            cols = slice(h * part, (h + 1) * part)
            first = lax.dot_general(left, i_q[:, cols], dims, preferred_element_type=jnp.float32)
            second = lax.dot_general(i_r[m], a_full[:, cols], dims, preferred_element_type=jnp.float32)
            block = ((first + second) / (row_gap[:, None] + col_gap[cols][None, :])).astype(jnp.bfloat16)
            if m:
                block = lax.ppermute(block, "row", [(s, s ^ m) for s in range(n_row)])
            landed.append((m, h * part, block))
    for m, shift, block in landed[-1:] + landed[:-1]:
        out = lax.dynamic_update_slice_in_dim(out, block, (r ^ m) * local_width + shift, 1)
    return out


def solution(mesh):
    return jax.shard_map(
        local,
        mesh=mesh,
        in_specs=(P("col", "row"), P("row", "col"), P(None, "row"), P(), P()),
        out_specs=P(("row", "col"), None),
        check_vma=False,
    )
```
